256 devices in a mesh: grp: 8 (over x_hi, y), blk: 32 (over x_lo, z, core).
Axes of the slice: x: 4 (x_hi: 2, x_lo: 2; x = x_hi * 2 + x_lo), y: 4, z: 8, core: 2. Of those that a mesh axis runs over, the one named last changes fastest.
Arguments:
- tokens: bfloat16 [32768, 2048], P(('grp', 'blk')), may hold values from -6 to 6
- d_out: bfloat16 [32768, 2048], P(('grp', 'blk')), may hold values from -24 to 24
- expert_ids: int32 [32768, 6], P(('grp', 'blk')), may hold values from 0 to 31, all different within a row; in each aligned block of 128 rows (0 to 127, 128 to 255, ...) at most 26 rows name the same one
- gate_values: bfloat16 [32768, 6], P(('grp', 'blk')), may hold values from 0.049804688 to 0.44921875
- saved_gate_pre: bfloat16 [32768, 6, 704], P(('grp', 'blk')), may hold values from -6 to 6
- saved_up_pre: bfloat16 [32768, 6, 704], P(('grp', 'blk')), may hold values from -6 to 6
- w_gate: bfloat16 [32, 2048, 704], P('blk'), may hold values from -0.125 to 0.125
- w_up: bfloat16 [32, 2048, 704], P('blk'), may hold values from -0.125 to 0.125
- w_down: bfloat16 [32, 704, 2048], P('blk'), may hold values from -0.21875 to 0.21875
Outputs:
- d_tokens: bfloat16 [32768, 2048], P(('grp', 'blk'))
- d_w_gate: bfloat16 [32, 2048, 704], P('blk', 'grp')
- d_w_up: bfloat16 [32, 2048, 704], P('blk', 'grp')
- d_w_down: bfloat16 [32, 704, 2048], P('blk', None, 'grp')
The draws below stay inside these ranges and needn't reach their ends.
Inputs may be any that keep to these rules, and one draw needn't show every extreme that they name: `expert_ids`: within the 128 rows of one device no expert is named more than 26 times, a bound that some block reaches; the 6 ids of a token differ.
All inputs are finite; a program needn't handle non-finite values.
Results may differ from the reference program's by a relative error of at most 0.0057.
Values may be sent and summed in bfloat16 or wider, within the bound.
A program may use at most 192 MiB of HBM per device.

```python
import math
import jax
import jax.numpy as jnp
import numpy as np
from jax import lax

D = 2048
TOPK = 6
FFW = 704
TOK_DEV = 128
EXPERTS = 32
CAP = 26
TOKENS = 32768
N_GRP = 8
N_BLK = 32


def with_spikes(entries, own_key, source, target, shards_of, factor):
    owner, partner = [(jnp.arange(entries.shape[position]) // (entries.shape[position] // shards_of)).reshape([-1 if axis == position else 1 for axis in range(entries.ndim)]) for position in (source, target)]
    chosen = jax.random.permutation(own_key, shards_of)[partner]
    strong = (owner == chosen) | (owner == (partner + shards_of // 2) % shards_of)
    return jnp.where(strong, factor * entries, entries)


def block_scale(stream_key, extent, shards, least, largest):
    factor_of, own = 1.0, jax.random.fold_in(stream_key, 6)
    for axis_at, parts in shards:
        draws = jnp.exp(jax.random.uniform(jax.random.fold_in(own, axis_at), (parts,), jnp.float32, least / len(shards), largest / len(shards)))
        factor_of = factor_of * jnp.repeat(draws, extent[axis_at] // parts).reshape([-1 if axis == axis_at else 1 for axis in range(len(extent))])
    return factor_of


def routed_block(own_key, own, number, rows, amount, top, most, lean):
    order = jax.random.permutation(own_key, amount)
    packed, ordinary = load_shares(amount, rows * top, most, lean, True), load_shares(amount, rows * top, most, lean, False)
    places = jnp.arange(amount)

    def named(sizes, turn):
        used = int((sizes > 0).sum())
        fixed = max(1, used // 4)
        moved = fixed + (places - fixed + turn * (used - fixed)) % max(1, amount - fixed)
        return jnp.zeros((amount,), jnp.int32).at[order[jnp.where(places < fixed, places, moved)]].set(jnp.asarray(sizes, jnp.int32))

    sizes = jnp.where(number % 4 == 0, named(packed, number // 4), named(ordinary, number - number // 4 - 1))
    mixed = jax.random.permutation(jax.random.fold_in(own, 3), amount)
    giver, sink = mixed[0:amount // 2 * 2:2], mixed[1:amount // 2 * 2:2]
    room = jnp.minimum(sizes[giver] - 1, most - sizes[sink]) // 2
    room = jnp.where((giver == order[0]) | (sink == order[0]) | (sizes[sink] == 0), 0, jnp.maximum(room, 0))
    moved = jax.random.randint(jax.random.fold_in(own, 4), (amount // 2,), 0, 1 << 20) % (room + 1)
    sizes = sizes.at[giver].add(-moved).at[sink].add(moved)
    members = jnp.searchsorted(jnp.cumsum(sizes), jnp.arange(rows * top), side="right").astype(jnp.int32)
    grid = members.reshape(top, rows).T
    grid = grid[jax.random.permutation(jax.random.fold_in(own, 1), rows)]
    turn = jax.random.randint(jax.random.fold_in(own, 2), (rows, 1), 0, top)
    return jnp.take_along_axis(grid, (jnp.arange(top)[None, :] + turn) % top, axis=1)


def load_shares(amount, total, reach, slope, full):
    loads = [(1 << 20) // math.isqrt(grade ** slope) + 1 for grade in range(1, amount + 1)]
    largest = reach if full else min(reach, max(-(-total // amount), total * loads[0] // sum(loads)))
    least = 1 if total - largest >= amount - 1 else 0
    given, rest = [largest] + [least] * (amount - 1), total - largest - least * (amount - 1)
    while rest > 0:
        movable = [i for i in range(1, amount) if given[i] < largest] or [i for i in range(1, amount) if given[i] < reach]
        mass, remaining = sum([loads[i] for i in movable]), rest
        for i in movable:
            extra = min(reach - given[i], max(1, remaining * loads[i] // mass), rest)
            given[i] = given[i] + extra
            rest = rest - extra
    return np.array(given)


def normal_values(rng, dims, deviation, bound, pieces=(), held_as=jnp.bfloat16):
    result = jax.random.normal(rng, dims, jnp.float32) * deviation
    if len(pieces) > 0:
        result = block_scale(rng, dims, pieces, -0.22, 0.18) * result
    return jnp.clip(result, min=-bound, max=bound).astype(held_as)


def gaussian_with(own_key, extent, deviation, reach, cuts, heavy, held_as=jnp.bfloat16):
    values = deviation * jax.random.normal(own_key, extent, jnp.float32)
    if cuts:
        values = values * block_scale(own_key, extent, cuts, -0.22, 0.18)
    return jnp.clip(with_spikes(values, jax.random.fold_in(own_key, 3), *heavy), -reach, reach).astype(held_as)


def setup_inputs(seed: int = 0) -> dict:
    key_of = jax.random.split(jax.random.key(seed), 10)
    tokens = normal_values(key_of[0], (TOKENS, D), 1.0, 6.0, ((0, 256),))
    d_out = gaussian_with(key_of[1], (TOKENS, D), 1.0, 24.0, ((0, 256),), (0, 1, 256, 6.0))
    expert_ids_keys = jax.random.split(jax.random.fold_in(key_of[2], 1), TOKENS // TOK_DEV)
    expert_ids_turns = jax.random.permutation(jax.random.fold_in(key_of[2], 3), TOKENS // TOK_DEV)
    expert_ids = jax.vmap(lambda own, number: routed_block(jax.random.fold_in(key_of[2], 2), own, number, TOK_DEV, EXPERTS, TOPK, CAP, 2))(expert_ids_keys, expert_ids_turns).reshape((TOKENS, TOPK))
    gate_values = jnp.clip(0.049804688 + 0.39941406 * jax.random.uniform(key_of[3], (TOKENS, TOPK), jnp.float32) ** block_scale(key_of[3], (TOKENS, TOPK), ((0, 256),), -0.2, 0.2), 0.049804688, 0.44921875).astype(jnp.bfloat16)
    saved_gate_pre = normal_values(key_of[4], (TOKENS, TOPK, FFW), 1.0, 6.0, ((0, 256),))
    saved_up_pre = normal_values(key_of[5], (TOKENS, TOPK, FFW), 1.0, 6.0, ((0, 256),))
    w_gate = normal_values(key_of[6], (EXPERTS, D, FFW), D ** -0.5, 0.125, ((0, 32),))
    w_up = normal_values(key_of[7], (EXPERTS, D, FFW), D ** -0.5, 0.125, ((0, 32),))
    w_down = normal_values(key_of[8], (EXPERTS, FFW, D), FFW ** -0.5, 0.21875, ((0, 32),))
    return {"tokens": tokens, "d_out": d_out, "expert_ids": expert_ids, "gate_values": gate_values, "saved_gate_pre": saved_gate_pre, "saved_up_pre": saved_up_pre, "w_gate": w_gate, "w_up": w_up, "w_down": w_down}


def expert_backward(inputs, cotangents, weights, gate_pre, up_pre, gate_mat, up_mat, down_mat):
    sigmoid_gate = jax.nn.sigmoid(gate_pre)
    active = gate_pre * sigmoid_gate
    scaled_hidden = (weights[:, None] * active * up_pre).astype(jnp.bfloat16)
    back_hidden = weights[:, None] * jnp.dot(cotangents, down_mat.T, preferred_element_type=jnp.float32)
    grad_gate = (back_hidden * up_pre * sigmoid_gate * (1.0 + gate_pre * (1.0 - sigmoid_gate))).astype(jnp.bfloat16)
    grad_up = (back_hidden * active).astype(jnp.bfloat16)
    route_grad = (jnp.dot(grad_gate, gate_mat.T, preferred_element_type=jnp.float32)
                  + jnp.dot(grad_up, up_mat.T, preferred_element_type=jnp.float32)).astype(jnp.bfloat16)
    sum_gate = jnp.dot(inputs.T, grad_gate, preferred_element_type=jnp.float32)
    sum_up = jnp.dot(inputs.T, grad_up, preferred_element_type=jnp.float32)
    sum_down = jnp.dot(scaled_hidden.T, cotangents, preferred_element_type=jnp.float32)
    return route_grad, sum_gate, sum_up, sum_down


def reference(tokens, d_out, expert_ids, gate_values, saved_gate_pre, saved_up_pre, w_gate, w_up, w_down):
    routes_total = TOKENS * TOPK
    most_rows = N_GRP * N_BLK * CAP
    flat_ids = expert_ids.reshape(-1)
    flat_gate = gate_values.reshape(-1).astype(jnp.float32)
    flat_gate_pre = saved_gate_pre.reshape(routes_total, FFW)
    flat_up_pre = saved_up_pre.reshape(routes_total, FFW)

    def one_expert(grad_accum, expert):
        positions = jnp.nonzero(flat_ids == expert, size=most_rows, fill_value=routes_total)[0].astype(jnp.int32)
        present = positions < routes_total
        clipped = jnp.minimum(positions, routes_total - 1)
        owner = clipped // TOPK
        weights = jnp.where(present, flat_gate[clipped], jnp.zeros_like(flat_gate[clipped]))
        inputs = jnp.where(present[:, None], tokens[owner], jnp.zeros_like(tokens[owner]))
        cotangents = jnp.where(present[:, None], d_out[owner], jnp.zeros_like(d_out[owner]))
        gate_pre = flat_gate_pre[clipped].astype(jnp.float32)
        up_pre = flat_up_pre[clipped].astype(jnp.float32)
        route_grad, sum_gate, sum_up, sum_down = expert_backward(
            inputs, cotangents, weights, gate_pre, up_pre, w_gate[expert], w_up[expert], w_down[expert])
        route_grad = jnp.where(present[:, None], route_grad.astype(jnp.float32), jnp.zeros((most_rows, D), jnp.float32))
        grad_accum = grad_accum.at[owner].add(route_grad)
        return grad_accum, (sum_gate.astype(jnp.bfloat16), sum_up.astype(jnp.bfloat16), sum_down.astype(jnp.bfloat16))

    start_accum = jnp.zeros((TOKENS, D), jnp.float32)
    grad_accum, stacked = lax.scan(one_expert, start_accum, jnp.arange(EXPERTS, dtype=jnp.int32))
    return grad_accum.astype(jnp.bfloat16), stacked[0], stacked[1], stacked[2]
```

```python
import jax
import jax.numpy as jnp
from jax import lax
from jax.experimental import pallas as pl
from jax.experimental.pallas import tpu as pltpu
from jax.sharding import PartitionSpec as P

MESH = pl.DeviceIdType.MESH
RING = 8
NEAR = 4
HOPS = RING // 2
PAD = 32


def place():
    me = lax.axis_index("blk")
    return me // (2 * RING) * 2 + lax.rem(me, 2), lax.rem(me // 2, RING)


def at(near, z):
    return near // 2 * (2 * RING) + z * 2 + lax.rem(near, 2)


def wrap(z):
    return lax.rem(z + RING, RING)


def greet(peers):
    barrier = pltpu.get_barrier_semaphore()
    for peer in peers:
        pl.semaphore_signal(barrier, inc=1, device_id=peer, device_id_type=MESH)
    return barrier


def remote(src, dst, send, recv, peer):
    return pltpu.make_async_remote_copy(
        src_ref=src, dst_ref=dst, send_sem=send, recv_sem=recv, device_id=peer, device_id_type=MESH
    )


def spread_kernel(
    d_ref, t_ref, g_ref, pre_ref, rd_ref, rt_ref, rpre_ref, rg_ref,
    ring_d, ring_t, pick_d, pick_t, ring_s, ring_r, near_s, near_r, near_l, g_s, g_r, pre_s, pre_r, own_sem,
):
    near, z = place()
    me = lax.axis_index("blk")
    count = 2 * 2 * RING
    barrier = pltpu.get_barrier_semaphore()

    def hello(k, carry):
        pl.semaphore_signal(
            barrier, inc=1, device_id={"blk": lax.rem(me + k, count)}, device_id_type=MESH
        )
        return carry

    lax.fori_loop(1, count, hello, 0)
    pl.semaphore_wait(barrier, count - 1)

    own_refs, rings = (d_ref, t_ref), (ring_d, ring_t)
    picks, lands = (pick_d, pick_t), (rd_ref, rt_ref)
    half = d_ref.shape[0] // 2

    def hop(a, way, k):
        step = 1 if way == 0 else -1
        source = wrap(z - step * k)
        src = own_refs[a] if k == 0 else rings[a].at[source]
        dst = rings[a].at[source]
        if k == HOPS - 1:
            src = src.at[pl.ds(way * half, half)]
            dst = dst.at[pl.ds(way * half, half)]
        return remote(
            src, dst, ring_s.at[a, way, k], ring_r.at[a, way, k], {"blk": at(near, wrap(z + step))}
        )

    def g_copy(k):
        to = wrap(z + k)
        return remote(g_ref.at[to], rg_ref.at[z], g_s.at[k], g_r.at[k], {"blk": at(near, to)})

    def pre_copy(k):
        to = lax.rem(me + k, count)
        return remote(pre_ref.at[to], rpre_ref.at[near, z], pre_s.at[k], pre_r.at[k], {"blk": to})

    for a in range(2):
        for way in range(2):
            hop(a, way, 0).start()
    for k in range(1, RING):
        g_copy(k).start()
    own_g = pltpu.make_async_copy(g_ref.at[z], rg_ref.at[z], own_sem.at[0])
    own_g.start()
    own_pre = pltpu.make_async_copy(pre_ref.at[me], rpre_ref.at[near, z], own_sem.at[1])
    own_pre.start()

    def pre_start(k, carry):
        pre_copy(k).start()
        return carry

    lax.fori_loop(1, count, pre_start, 0)

    def near_copy(a, source, number, j):
        to = lax.rem(near + j, NEAR)
        src = picks[a].at[source, to]
        if j == 0:
            return pltpu.make_async_copy(src, lands[a].at[near, source], near_l.at[a, number])
        return remote(
            src, lands[a].at[near, source], near_s.at[a, number, j], near_r.at[a, number, j],
            {"blk": at(to, z)},
        )

    def gather(a, source, number):
        rows = own_refs[a][...] if number == 0 else rings[a][source]
        taken = jnp.dot(rg_ref[source], rows, preferred_element_type=jnp.float32)
        picks[a][source] = taken.astype(jnp.bfloat16).reshape(NEAR, PAD, taken.shape[1])
        for j in (1, 2, 3, 0):
            near_copy(a, source, number, j).start()

    own_g.wait()
    for a in range(2):
        gather(a, z, 0)
    for k in range(1, RING):
        g_copy(k).wait()
    for k in range(HOPS):
        for a in range(2):
            for way in range(2):
                hop(a, way, k).wait_recv()
                if k + 1 < HOPS:
                    hop(a, way, k + 1).start()
            if k + 1 < HOPS:
                gather(a, wrap(z - k - 1), 2 * k + 1)
                gather(a, wrap(z + k + 1), 2 * k + 2)
            else:
                gather(a, wrap(z + HOPS), 2 * k + 1)

    own_pre.wait()

    def pre_wait(k, carry):
        pre_copy(k).wait()
        return carry

    lax.fori_loop(1, count, pre_wait, 0)
    for a in range(2):
        for way in range(2):
            for k in range(HOPS):
                hop(a, way, k).wait_send()
        for number in range(RING):
            offset = (number + 1) // 2
            source = wrap(z - offset if number % 2 else z + offset)
            for j in range(NEAR):
                near_copy(a, source, number, j).wait()


def fold_kernel(
    ret_ref, g_ref, w_ref, out_ref, rw_ref,
    land, part, ring, near_s, near_r, near_l, ring_s, ring_r, w_s, w_r,
):
    near, z = place()
    grp = lax.axis_index("grp")
    groups = lax.axis_size("grp")
    width = w_ref.shape[2] // groups
    barrier = greet(
        [{"grp": lax.rem(grp + j, groups)} for j in range(1, groups)]
        + [{"blk": at(lax.rem(near + j, NEAR), z)} for j in range(1, NEAR)]
        + [{"blk": at(near, wrap(z + step))} for step in (1, -1)]
    )
    pl.semaphore_wait(barrier, groups + NEAR)

    def near_copy(number, j):
        offset = (number + 1) // 2
        source = wrap(z - offset if number % 2 else z + offset)
        to = lax.rem(near + j, NEAR)
        src, dst = ret_ref.at[to, source], land.at[source, near]
        if j == 0:
            return pltpu.make_async_copy(src, dst, near_l.at[number])
        return remote(src, dst, near_s.at[number, j], near_r.at[number, j], {"blk": at(to, z)})

    def w_copy(j):
        to = lax.rem(grp + j, groups)
        cols = pl.ds(pl.multiple_of(to * width, width), width)
        return remote(w_ref.at[:, :, cols], rw_ref.at[j - 1], w_s.at[j], w_r.at[j], {"grp": to})

    for number in reversed(range(RING)):
        for j in (1, 2, 3, 0):
            near_copy(number, j).start()
    for j in range(1, groups):
        w_copy(j).start()

    half = out_ref.shape[0] // 2

    def hop(way, k):
        step = 1 if way == 0 else -1
        src, dst = part.at[way, k], ring.at[way, k]
        if k == 0:
            src, dst = src.at[pl.ds(0, half)], dst.at[pl.ds(0, half)]
        return remote(src, dst, ring_s.at[way, k], ring_r.at[way, k], {"blk": at(near, wrap(z + step))})

    def scattered(number):
        offset = (number + 1) // 2
        source = wrap(z - offset if number % 2 else z + offset)
        for j in range(NEAR):
            near_copy(number, j).wait()
        rows = land[source].reshape(NEAR * PAD, out_ref.shape[1])
        return jnp.dot(g_ref[source], rows, preferred_element_type=jnp.float32)

    far = scattered(RING - 1).astype(jnp.bfloat16)
    for way in range(2):
        part[way, 0, 0:half] = far[way * half : (way + 1) * half]
        hop(way, 0).start()
    for k in range(1, HOPS):
        for way in range(2):
            offset = HOPS - k
            own = scattered(2 * offset if way == 0 else 2 * offset - 1)
            hop(way, k - 1).wait_recv()
            if k == 1:
                low = ring[way, 0, 0:half].astype(jnp.float32)
                rows = slice(way * half, (way + 1) * half)
                part[way, k] = own.astype(jnp.bfloat16)
                part[way, k, rows] = (own[rows] + low).astype(jnp.bfloat16)
            else:
                part[way, k] = (own + ring[way, k - 1].astype(jnp.float32)).astype(jnp.bfloat16)
            hop(way, k).start()
    own = scattered(0)
    for way in range(2):
        hop(way, HOPS - 1).wait_recv()
        own = own + ring[way, HOPS - 1].astype(jnp.float32)
    out_ref[...] = own.astype(jnp.bfloat16)
    for way in range(2):
        for k in range(HOPS):
            hop(way, k).wait_send()
    for j in range(1, groups):
        w_copy(j).wait()


def spread(d_out, tokens, onehot, pre):
    rows, width = d_out.shape
    bf16, dma = jnp.bfloat16, pltpu.SemaphoreType.DMA
    vmem, anywhere = pl.BlockSpec(memory_space=pltpu.VMEM), pl.BlockSpec(memory_space=pl.ANY)
    landed = jax.ShapeDtypeStruct((NEAR, RING, PAD, width), bf16)
    return pl.pallas_call(
        spread_kernel,
        out_shape=(
            landed,
            landed,
            jax.ShapeDtypeStruct((NEAR, RING) + pre.shape[1:], bf16),
            jax.ShapeDtypeStruct(onehot.shape, bf16),
        ),
        in_specs=[vmem, vmem, vmem, anywhere],
        out_specs=(vmem, vmem, anywhere, vmem),
        scratch_shapes=[
            pltpu.VMEM((RING, rows, width), bf16),
            pltpu.VMEM((RING, rows, width), bf16),
            pltpu.VMEM((RING, NEAR, PAD, width), bf16),
            pltpu.VMEM((RING, NEAR, PAD, width), bf16),
            dma((2, 2, HOPS)),
            dma((2, 2, HOPS)),
            dma((2, RING, NEAR)),
            dma((2, RING, NEAR)),
            dma((2, RING)),
            dma((RING,)),
            dma((RING,)),
            dma((NEAR * RING,)),
            dma((NEAR * RING,)),
            dma((2,)),
        ],
        compiler_params=pltpu.CompilerParams(
            collective_id=0, has_side_effects=True, vmem_limit_bytes=48 << 20
        ),
        name="spread",
    )(d_out, tokens, onehot, pre)


def fold(ret, onehot_t, terms):
    width = ret.shape[-1]
    rows = onehot_t.shape[1]
    bf16, dma = jnp.bfloat16, pltpu.SemaphoreType.DMA
    vmem, anywhere = pl.BlockSpec(memory_space=pltpu.VMEM), pl.BlockSpec(memory_space=pl.ANY)
    groups = lax.axis_size("grp")
    return pl.pallas_call(
        fold_kernel,
        out_shape=(
            jax.ShapeDtypeStruct((rows, width), bf16),
            jax.ShapeDtypeStruct((groups - 1,) + terms.shape[:2] + (terms.shape[2] // groups,), bf16),
        ),
        in_specs=[vmem, vmem, anywhere],
        out_specs=(vmem, anywhere),
        scratch_shapes=[
            pltpu.VMEM((RING, NEAR, PAD, width), bf16),
            pltpu.VMEM((2, HOPS, rows, width), bf16),
            pltpu.VMEM((2, HOPS, rows, width), bf16),
            dma((RING, NEAR)),
            dma((RING, NEAR)),
            dma((RING,)),
            dma((2, HOPS)),
            dma((2, HOPS)),
            dma((groups,)),
            dma((groups,)),
        ],
        compiler_params=pltpu.CompilerParams(
            collective_id=1, has_side_effects=True, vmem_limit_bytes=48 << 20
        ),
        name="fold",
    )(ret, onehot_t, terms)


def per_device(
    tokens, d_out, expert_ids, gate_values, saved_gate_pre, saved_up_pre, w_gate, w_up, w_down
):
    bf16, f32 = jnp.bfloat16, jnp.float32
    rows, width = tokens.shape
    ffw = saved_gate_pre.shape[2]
    experts = NEAR * RING
    chosen = expert_ids[:, :, None] == jnp.arange(experts, dtype=jnp.int32)[None, None, :]
    hit = jnp.any(chosen, axis=1)
    before = jnp.tril(jnp.ones((rows, rows), bf16), -1)
    rank = jnp.dot(before, hit.astype(bf16), preferred_element_type=f32).astype(jnp.int32)
    slot = jnp.where(hit, rank, PAD).T
    onehot = (slot[:, None, :] == jnp.arange(PAD, dtype=jnp.int32)[None, :, None])
    by_z = onehot.astype(bf16).reshape(2, RING, 2, PAD, rows)
    by_z = jnp.transpose(by_z, (1, 0, 2, 3, 4)).reshape(RING, NEAR * PAD, rows)
    route = (onehot[None] & chosen.transpose(1, 2, 0)[:, :, None, :]).astype(bf16)
    route = route.reshape(-1, experts * PAD, rows)
    picked = [
        jnp.einsum("kst,tkf->sf", route, table, preferred_element_type=bf16)
        for table in (saved_gate_pre, saved_up_pre)
    ]
    gate_of = jnp.sum(jnp.where(chosen, gate_values.astype(f32)[:, :, None], 0.0), axis=1).T
    gate_slot = jnp.sum(jnp.where(onehot, gate_of[:, None, :], 0.0), axis=2)
    pre = jnp.concatenate(picked, axis=1).reshape(experts, PAD, 2 * ffw)
    slots = 13 * rows // (2 * experts)
    pre = pre + jnp.pad(
        gate_slot.astype(bf16)[:, None, :], ((0, 0), (slots, PAD - slots - 1), (0, 2 * ffw - PAD))
    )

    recv_d, recv_t, recv_pre, recv_g = spread(d_out, tokens, by_z, pre)

    cot = recv_d.reshape(experts * PAD, width)
    inputs = recv_t.reshape(experts * PAD, width)
    weights = recv_pre[:, :, slots, :PAD].astype(f32).reshape(experts * PAD, 1)
    recv_pre = recv_pre.reshape(experts * PAD, 2 * ffw)
    gate_pre = recv_pre[:, :ffw].astype(f32)
    up_pre = recv_pre[:, ffw:].astype(f32)
    sig = jax.nn.sigmoid(gate_pre)
    active = gate_pre * sig
    hidden = (weights * active * up_pre).astype(bf16)
    back = weights * jnp.einsum("rd,fd->rf", cot, w_down[0], preferred_element_type=f32)
    grad_gate = (back * up_pre * sig * (1.0 + gate_pre * (1.0 - sig))).astype(bf16)
    grad_up = (back * active).astype(bf16)
    ret = (
        jnp.einsum("rf,df->rd", grad_gate, w_gate[0], preferred_element_type=f32)
        + jnp.einsum("rf,df->rd", grad_up, w_up[0], preferred_element_type=f32)
    ).astype(bf16)
    terms = jnp.stack(
        [
            jnp.einsum("rf,rd->fd", left, right, preferred_element_type=f32).astype(bf16)
            for left, right in ((grad_gate, inputs), (grad_up, inputs), (hidden, cot))
        ]
    )

    d_tokens, got = fold(
        ret.reshape(NEAR, RING, PAD, width), jnp.swapaxes(recv_g, 1, 2), terms
    )
    mine = lax.dynamic_slice_in_dim(
        terms, lax.axis_index("grp") * got.shape[3], got.shape[3], axis=2
    )
    sums = (jnp.sum(got.astype(f32), axis=0) + mine.astype(f32)).astype(bf16)
    return (
        d_tokens,
        jnp.swapaxes(sums[0], 0, 1)[None],
        jnp.swapaxes(sums[1], 0, 1)[None],
        sums[2][None],
    )


def solution(mesh):
    rows = P(("grp", "blk"), None)
    return jax.shard_map(
        per_device,
        mesh=mesh,
        in_specs=(
            rows,
            rows,
            rows,
            rows,
            P(("grp", "blk"), None, None),
            P(("grp", "blk"), None, None),
            P("blk", None, None),
            P("blk", None, None),
            P("blk", None, None),
        ),
        out_specs=(rows, P("blk", "grp", None), P("blk", "grp", None), P("blk", None, "grp")),
        check_vma=False,
    )
```

```python
import jax
import jax.numpy as jnp
from jax import lax
from jax.experimental import pallas as pl
from jax.experimental.pallas import tpu as pltpu
from jax.sharding import PartitionSpec as P

MESH = pl.DeviceIdType.MESH
RING = 8
NEAR = 4
HOPS = RING // 2
PAD = 32
SIDE = 4


def place():
    me = lax.axis_index("blk")
    return me // (2 * RING) * 2 + lax.rem(me, 2), lax.rem(me // 2, RING)


def at(near, z):
    return near // 2 * (2 * RING) + z * 2 + lax.rem(near, 2)


def wrap(z):
    return lax.rem(z + RING, RING)


def turn(y):
    return lax.rem(y + 2 * SIDE, SIDE)


def greet(peers):
    barrier = pltpu.get_barrier_semaphore()
    for peer in peers:
        pl.semaphore_signal(barrier, inc=1, device_id=peer, device_id_type=MESH)
    return barrier


def remote(src, dst, send, recv, peer):
    return pltpu.make_async_remote_copy(
        src_ref=src, dst_ref=dst, send_sem=send, recv_sem=recv, device_id=peer, device_id_type=MESH
    )


def spread_kernel(
    d_ref, t_ref, g_ref, pre_ref, rd_ref, rt_ref, rpre_ref, rg_ref,
    ring_d, ring_t, pick_d, pick_t, ring_s, ring_r, near_s, near_r, near_l, g_s, g_r, pre_s, pre_r, own_sem,
):
    near, z = place()
    me = lax.axis_index("blk")
    count = 2 * 2 * RING
    barrier = pltpu.get_barrier_semaphore()

    def hello(k, carry):
        pl.semaphore_signal(
            barrier, inc=1, device_id={"blk": lax.rem(me + k, count)}, device_id_type=MESH
        )
        return carry

    lax.fori_loop(1, count, hello, 0)
    pl.semaphore_wait(barrier, count - 1)

    own_refs, rings = (d_ref, t_ref), (ring_d, ring_t)
    picks, lands = (pick_d, pick_t), (rd_ref, rt_ref)
    half = d_ref.shape[0] // 2

    def hop(a, way, k):
        step = 1 if way == 0 else -1
        source = wrap(z - step * k)
        src = own_refs[a] if k == 0 else rings[a].at[source]
        dst = rings[a].at[source]
        if k == HOPS - 1:
            src = src.at[pl.ds(way * half, half)]
            dst = dst.at[pl.ds(way * half, half)]
        return remote(
            src, dst, ring_s.at[a, way, k], ring_r.at[a, way, k], {"blk": at(near, wrap(z + step))}
        )

    def g_copy(k):
        to = wrap(z + k)
        return remote(g_ref.at[to], rg_ref.at[z], g_s.at[k], g_r.at[k], {"blk": at(near, to)})

    def pre_copy(k):
        to = lax.rem(me + k, count)
        return remote(pre_ref.at[to], rpre_ref.at[near, z], pre_s.at[k], pre_r.at[k], {"blk": to})

    for a in range(2):
        for way in range(2):
            hop(a, way, 0).start()
    for k in range(1, RING):
        g_copy(k).start()
    own_g = pltpu.make_async_copy(g_ref.at[z], rg_ref.at[z], own_sem.at[0])
    own_g.start()
    own_pre = pltpu.make_async_copy(pre_ref.at[me], rpre_ref.at[near, z], own_sem.at[1])
    own_pre.start()

    def pre_start(k, carry):
        pre_copy(k).start()
        return carry

    lax.fori_loop(1, count, pre_start, 0)

    def near_copy(a, source, number, j):
        to = lax.rem(near + j, NEAR)
        src = picks[a].at[source, to]
        if j == 0:
            return pltpu.make_async_copy(src, lands[a].at[near, source], near_l.at[a, number])
        return remote(
            src, lands[a].at[near, source], near_s.at[a, number, j], near_r.at[a, number, j],
            {"blk": at(to, z)},
        )

    def gather(a, source, number):
        rows = own_refs[a][...] if number == 0 else rings[a][source]
        taken = jnp.dot(rg_ref[source], rows, preferred_element_type=jnp.float32)
        picks[a][source] = taken.astype(jnp.bfloat16).reshape(NEAR, PAD, taken.shape[1])
        for j in (1, 2, 3, 0):
            near_copy(a, source, number, j).start()

    own_g.wait()
    for a in range(2):
        gather(a, z, 0)
    for k in range(1, RING):
        g_copy(k).wait()
    for k in range(HOPS):
        for a in range(2):
            for way in range(2):
                hop(a, way, k).wait_recv()
                if k + 1 < HOPS:
                    hop(a, way, k + 1).start()
            if k + 1 < HOPS:
                gather(a, wrap(z - k - 1), 2 * k + 1)
                gather(a, wrap(z + k + 1), 2 * k + 2)
            else:
                gather(a, wrap(z + HOPS), 2 * k + 1)

    own_pre.wait()

    def pre_wait(k, carry):
        pre_copy(k).wait()
        return carry

    lax.fori_loop(1, count, pre_wait, 0)
    for a in range(2):
        for way in range(2):
            for k in range(HOPS):
                hop(a, way, k).wait_send()
        for number in range(RING):
            offset = (number + 1) // 2
            source = wrap(z - offset if number % 2 else z + offset)
            for j in range(NEAR):
                near_copy(a, source, number, j).wait()


def fold_kernel(
    ret_ref, g_ref, wg_ref, wu_ref, wd_ref, out_ref, sg_ref, su_ref, sd_ref,
    land, part, ring, own_w, acc, cross, near_s, near_r, near_l, ring_s, ring_r, own_sem, w_s, w_r, x_s, x_r,
):
    near, z = place()
    grp = lax.axis_index("grp")
    side, y = grp // SIDE, lax.rem(grp, SIDE)
    other = 1 - side
    terms, sums = (wg_ref, wu_ref, wd_ref), (sg_ref, su_ref, sd_ref)
    width = sg_ref.shape[1]
    barrier = greet(
        [{"grp": side * SIDE + turn(y + step)} for step in (1, -1)]
        + [{"grp": other * SIDE + y}]
        + [{"blk": at(lax.rem(near + j, NEAR), z)} for j in range(1, NEAR)]
        + [{"blk": at(near, wrap(z + step))} for step in (1, -1)]
    )
    pl.semaphore_wait(barrier, 5 + NEAR - 1)

    def near_copy(number, j):
        offset = (number + 1) // 2
        source = wrap(z - offset if number % 2 else z + offset)
        to = lax.rem(near + j, NEAR)
        src, dst = ret_ref.at[to, source], land.at[source, near]
        if j == 0:
            return pltpu.make_async_copy(src, dst, near_l.at[number])
        return remote(src, dst, near_s.at[number, j], near_r.at[number, j], {"blk": at(to, z)})

    def cols(way, to):
        start = ((other if way == 0 else side) * SIDE + to) * width
        return pl.ds(pl.multiple_of(start, width), width)

    def w_hop(way, k, t):
        step = 1 if way == 0 else -1
        src = terms[t].at[:, cols(way, turn(y - step))] if k == 0 else acc.at[way, k - 1, t]
        return remote(
            src, acc.at[way, k, t], w_s.at[way, k, t], w_r.at[way, k, t],
            {"grp": side * SIDE + turn(y + step)},
        )

    def x_copy(t):
        return remote(acc.at[0, SIDE - 2, t], cross.at[t], x_s.at[t], x_r.at[t], {"grp": other * SIDE + y})

    def own_copy(t):
        return pltpu.make_async_copy(terms[t], own_w.at[t], own_sem.at[t])

    def w_sum(way, k, t):
        step = 1 if way == 0 else -1
        w_hop(way, k, t).wait_recv()
        own = own_w[t, :, cols(way, turn(y - step * (k + 2)))]
        return acc[way, k, t].astype(jnp.float32) + own.astype(jnp.float32)

    def w_turn(k):
        for t in range(3):
            for way in range(2):
                acc[way, k, t] = w_sum(way, k, t).astype(jnp.bfloat16)
                w_hop(way, k + 1, t).start()

    for t in range(3):
        for way in range(2):
            w_hop(way, 0, t).start()
    for number in reversed(range(RING)):
        for j in (1, 2, 3, 0):
            near_copy(number, j).start()
    for t in range(3):
        own_copy(t).start()

    half = out_ref.shape[0] // 2

    def hop(way, k):
        step = 1 if way == 0 else -1
        src, dst = part.at[way, k], ring.at[way, k]
        if k == 0:
            src, dst = src.at[pl.ds(0, half)], dst.at[pl.ds(0, half)]
        return remote(src, dst, ring_s.at[way, k], ring_r.at[way, k], {"blk": at(near, wrap(z + step))})

    def scattered(number):
        offset = (number + 1) // 2
        source = wrap(z - offset if number % 2 else z + offset)
        for j in range(NEAR):
            near_copy(number, j).wait()
        rows = land[source].reshape(NEAR * PAD, out_ref.shape[1])
        return jnp.dot(g_ref[source], rows, preferred_element_type=jnp.float32)

    far = scattered(RING - 1).astype(jnp.bfloat16)
    for way in range(2):
        part[way, 0, 0:half] = far[way * half : (way + 1) * half]
        hop(way, 0).start()
    for t in range(3):
        own_copy(t).wait()
    for k in range(1, HOPS):
        for way in range(2):
            offset = HOPS - k
            own = scattered(2 * offset if way == 0 else 2 * offset - 1)
            hop(way, k - 1).wait_recv()
            if k == 1:
                low = ring[way, 0, 0:half].astype(jnp.float32)
                rows = slice(way * half, (way + 1) * half)
                part[way, k] = own.astype(jnp.bfloat16)
                part[way, k, rows] = (own[rows] + low).astype(jnp.bfloat16)
            else:
                part[way, k] = (own + ring[way, k - 1].astype(jnp.float32)).astype(jnp.bfloat16)
            hop(way, k).start()
        if k == 1:
            w_turn(0)
    w_turn(1)
    own = scattered(0)
    for way in range(2):
        hop(way, HOPS - 1).wait_recv()
        own = own + ring[way, HOPS - 1].astype(jnp.float32)
    out_ref[...] = own.astype(jnp.bfloat16)
    for t in range(3):
        acc[0, SIDE - 2, t] = w_sum(0, SIDE - 2, t).astype(jnp.bfloat16)
        x_copy(t).start()
    for t in range(3):
        mine = w_sum(1, SIDE - 2, t)
        x_copy(t).wait_recv()
        sums[t][...] = (mine + cross[t].astype(jnp.float32)).astype(jnp.bfloat16)
    for way in range(2):
        for k in range(HOPS):
            hop(way, k).wait_send()
        for k in range(SIDE - 1):
            for t in range(3):
                w_hop(way, k, t).wait_send()
    for t in range(3):
        x_copy(t).wait_send()


def spread(d_out, tokens, onehot, pre):
    rows, width = d_out.shape
    bf16, dma = jnp.bfloat16, pltpu.SemaphoreType.DMA
    vmem, anywhere = pl.BlockSpec(memory_space=pltpu.VMEM), pl.BlockSpec(memory_space=pl.ANY)
    landed = jax.ShapeDtypeStruct((NEAR, RING, PAD, width), bf16)
    return pl.pallas_call(
        spread_kernel,
        out_shape=(
            landed,
            landed,
            jax.ShapeDtypeStruct((NEAR, RING) + pre.shape[1:], bf16),
            jax.ShapeDtypeStruct(onehot.shape, bf16),
        ),
        in_specs=[vmem, vmem, vmem, anywhere],
        out_specs=(vmem, vmem, anywhere, vmem),
        scratch_shapes=[
            pltpu.VMEM((RING, rows, width), bf16),
            pltpu.VMEM((RING, rows, width), bf16),
            pltpu.VMEM((RING, NEAR, PAD, width), bf16),
            pltpu.VMEM((RING, NEAR, PAD, width), bf16),
            dma((2, 2, HOPS)),
            dma((2, 2, HOPS)),
            dma((2, RING, NEAR)),
            dma((2, RING, NEAR)),
            dma((2, RING)),
            dma((RING,)),
            dma((RING,)),
            dma((NEAR * RING,)),
            dma((NEAR * RING,)),
            dma((2,)),
        ],
        compiler_params=pltpu.CompilerParams(
            collective_id=0, has_side_effects=True, vmem_limit_bytes=48 << 20
        ),
        name="spread",
    )(d_out, tokens, onehot, pre)


def fold(ret, onehot_t, terms):
    width = ret.shape[-1]
    rows = onehot_t.shape[1]
    bf16, dma = jnp.bfloat16, pltpu.SemaphoreType.DMA
    vmem, anywhere = pl.BlockSpec(memory_space=pltpu.VMEM), pl.BlockSpec(memory_space=pl.ANY)
    ffw = terms[0].shape[0]
    share = (ffw, width // lax.axis_size("grp"))
    return pl.pallas_call(
        fold_kernel,
        out_shape=(jax.ShapeDtypeStruct((rows, width), bf16),) + (jax.ShapeDtypeStruct(share, bf16),) * 3,
        in_specs=[vmem, vmem, anywhere, anywhere, anywhere],
        out_specs=(vmem,) * 4,
        scratch_shapes=[
            pltpu.VMEM((RING, NEAR, PAD, width), bf16),
            pltpu.VMEM((2, HOPS, rows, width), bf16),
            pltpu.VMEM((2, HOPS, rows, width), bf16),
            pltpu.VMEM((3, ffw, width), bf16),
            pltpu.VMEM((2, SIDE - 1, 3) + share, bf16),
            pltpu.VMEM((3,) + share, bf16),
            dma((RING, NEAR)),
            dma((RING, NEAR)),
            dma((RING,)),
            dma((2, HOPS)),
            dma((2, HOPS)),
            dma((3,)),
            dma((2, SIDE - 1, 3)),
            dma((2, SIDE - 1, 3)),
            dma((3,)),
            dma((3,)),
        ],
        compiler_params=pltpu.CompilerParams(
            collective_id=1, has_side_effects=True, vmem_limit_bytes=48 << 20
        ),
        name="fold",
    )(ret, onehot_t, *terms)


def per_device(
    tokens, d_out, expert_ids, gate_values, saved_gate_pre, saved_up_pre, w_gate, w_up, w_down
):
    bf16, f32 = jnp.bfloat16, jnp.float32
    rows, width = tokens.shape
    ffw = saved_gate_pre.shape[2]
    experts = NEAR * RING
    chosen = expert_ids[:, :, None] == jnp.arange(experts, dtype=jnp.int32)[None, None, :]
    hit = jnp.any(chosen, axis=1)
    before = jnp.tril(jnp.ones((rows, rows), bf16), -1)
    rank = jnp.dot(before, hit.astype(bf16), preferred_element_type=f32).astype(jnp.int32)
    slot = jnp.where(hit, rank, PAD).T
    onehot = (slot[:, None, :] == jnp.arange(PAD, dtype=jnp.int32)[None, :, None])
    by_z = onehot.astype(bf16).reshape(2, RING, 2, PAD, rows)
    by_z = jnp.transpose(by_z, (1, 0, 2, 3, 4)).reshape(RING, NEAR * PAD, rows)
    route = (onehot[None] & chosen.transpose(1, 2, 0)[:, :, None, :]).astype(bf16)
    route = route.reshape(-1, experts * PAD, rows)
    picked = [
        jnp.einsum("kst,tkf->sf", route, table, preferred_element_type=bf16)
        for table in (saved_gate_pre, saved_up_pre)
    ]
    gate_of = jnp.sum(jnp.where(chosen, gate_values.astype(f32)[:, :, None], 0.0), axis=1).T
    gate_slot = jnp.sum(jnp.where(onehot, gate_of[:, None, :], 0.0), axis=2)
    pre = jnp.concatenate(picked, axis=1).reshape(experts, PAD, 2 * ffw)
    slots = 13 * rows // (2 * experts)
    pre = pre + jnp.pad(
        gate_slot.astype(bf16)[:, None, :], ((0, 0), (slots, PAD - slots - 1), (0, 2 * ffw - PAD))
    )

    recv_d, recv_t, recv_pre, recv_g = spread(d_out, tokens, by_z, pre)

    cot = recv_d.reshape(experts * PAD, width)
    inputs = recv_t.reshape(experts * PAD, width)
    weights = recv_pre[:, :, slots, :PAD].astype(f32).reshape(experts * PAD, 1)
    recv_pre = recv_pre.reshape(experts * PAD, 2 * ffw)
    gate_pre = recv_pre[:, :ffw].astype(f32)
    up_pre = recv_pre[:, ffw:].astype(f32)
    sig = jax.nn.sigmoid(gate_pre)
    active = gate_pre * sig
    hidden = (weights * active * up_pre).astype(bf16)
    back = weights * jnp.einsum("rd,fd->rf", cot, w_down[0], preferred_element_type=f32)
    grad_gate = (back * up_pre * sig * (1.0 + gate_pre * (1.0 - sig))).astype(bf16)
    grad_up = (back * active).astype(bf16)
    ret = (
        jnp.einsum("rf,df->rd", grad_gate, w_gate[0], preferred_element_type=f32)
        + jnp.einsum("rf,df->rd", grad_up, w_up[0], preferred_element_type=f32)
    ).astype(bf16)
    terms = [
        jnp.einsum("rf,rd->fd", left, right, preferred_element_type=f32).astype(bf16)
        for left, right in ((grad_gate, inputs), (grad_up, inputs), (hidden, cot))
    ]

    d_tokens, sum_gate, sum_up, sum_down = fold(
        ret.reshape(NEAR, RING, PAD, width), jnp.swapaxes(recv_g, 1, 2), terms
    )
    return (
        d_tokens,
        jnp.swapaxes(sum_gate, 0, 1)[None],
        jnp.swapaxes(sum_up, 0, 1)[None],
        sum_down[None],
    )


def solution(mesh):
    rows = P(("grp", "blk"), None)
    return jax.shard_map(
        per_device,
        mesh=mesh,
        in_specs=(
            rows,
            rows,
            rows,
            rows,
            P(("grp", "blk"), None, None),
            P(("grp", "blk"), None, None),
            P("blk", None, None),
            P("blk", None, None),
            P("blk", None, None),
        ),
        out_specs=(rows, P("blk", "grp", None), P("blk", "grp", None), P("blk", None, "grp")),
        check_vma=False,
    )
```

```python
import jax
import jax.numpy as jnp
from jax import lax
from jax.experimental import pallas as pl
from jax.experimental.pallas import tpu as pltpu
from jax.sharding import PartitionSpec as P

MESH = pl.DeviceIdType.MESH
RING = 8
NEAR = 4
HOPS = RING // 2
PAD = 32
LOW = 64
PRE_STAGES = ((3, 5), (4,), (2, 6), (1, 7, 0))
SIDE = 4


def place():
    me = lax.axis_index("blk")
    return me // (2 * RING) * 2 + lax.rem(me, 2), lax.rem(me // 2, RING)


def at(near, z):
    return near // 2 * (2 * RING) + z * 2 + lax.rem(near, 2)


def wrap(z):
    return lax.rem(z + RING, RING)


def turn(y):
    return lax.rem(y + 2 * SIDE, SIDE)


def greet(peers):
    barrier = pltpu.get_barrier_semaphore()
    for peer in peers:
        pl.semaphore_signal(barrier, inc=1, device_id=peer, device_id_type=MESH)
    return barrier


def remote(src, dst, send, recv, peer):
    return pltpu.make_async_remote_copy(
        src_ref=src, dst_ref=dst, send_sem=send, recv_sem=recv, device_id=peer, device_id_type=MESH
    )


def spread_kernel(
    d_ref, t_ref, g_ref, route_ref, gate_ref, up_ref, rd_ref, rt_ref, rpre_ref, rg_ref,
    table, pre, table_sem, ring_d, ring_t, pick_d, pick_t, ring_s, ring_r, near_s, near_r, near_l, g_s, g_r, pre_s, pre_r, own_sem,
):
    near, z = place()
    me = lax.axis_index("blk")
    count = 2 * 2 * RING
    barrier = pltpu.get_barrier_semaphore()

    def hello(k, carry):
        pl.semaphore_signal(
            barrier, inc=1, device_id={"blk": lax.rem(me + k, count)}, device_id_type=MESH
        )
        return carry

    lax.fori_loop(1, count, hello, 0)
    pl.semaphore_wait(barrier, count - 1)

    own_refs, rings = (d_ref, t_ref), (ring_d, ring_t)
    picks, lands = (pick_d, pick_t), (rd_ref, rt_ref)
    far = pl.ds(0, LOW), pl.ds(LOW, d_ref.shape[0] - LOW)

    def ways(k):
        return [way for way in range(2) if k < HOPS - 1 or far[way].size]

    def hop(a, way, k):
        step = 1 if way == 0 else -1
        source = wrap(z - step * k)
        src = own_refs[a] if k == 0 else rings[a].at[source]
        dst = rings[a].at[source]
        if k == HOPS - 1:
            src = src.at[far[way]]
            dst = dst.at[far[way]]
        return remote(
            src, dst, ring_s.at[a, way, k], ring_r.at[a, way, k], {"blk": at(near, wrap(z + step))}
        )

    def g_copy(k):
        to = wrap(z + k)
        return remote(g_ref.at[to], rg_ref.at[z], g_s.at[k], g_r.at[k], {"blk": at(near, to)})

    def pre_copy(k, j):
        to = at(lax.rem(near + j, NEAR), wrap(z + k))
        return remote(pre.at[to], rpre_ref.at[near, z], pre_s.at[k, j], pre_r.at[k, j], {"blk": to})

    def pre_each(number, act):
        for k in PRE_STAGES[number]:
            def one(j, carry, k=k):
                act(pre_copy(k, j))
                return carry

            lax.fori_loop(0 if k else 1, NEAR, one, 0)

    choices, ffw, rows = gate_ref.shape

    def table_copy(i, k):
        ref = (gate_ref, up_ref)[i]
        dst = table.at[pl.ds(i * ffw, ffw), pl.ds(k * rows, rows)]
        return pltpu.make_async_copy(ref.at[k], dst, table_sem.at[i, k])

    for a in range(2):
        for way in range(2):
            hop(a, way, 0).start()
    for i in range(2):
        for k in range(choices):
            table_copy(i, k).start()
    for k in range(1, RING):
        g_copy(k).start()
    own_g = pltpu.make_async_copy(g_ref.at[z], rg_ref.at[z], own_sem.at[0])
    own_g.start()
    for i in range(2):
        for k in range(choices):
            table_copy(i, k).wait()

    def build(i, carry):
        slots = pl.ds(pl.multiple_of(i * 8 * PAD, 8 * PAD), 8 * PAD)
        take = jnp.concatenate([route_ref[k, slots, :] for k in range(choices)], axis=1)
        taken = lax.dot_general(
            take, table[...], (((1,), (1,)), ((), ())), preferred_element_type=jnp.float32
        )
        pre[pl.ds(i * 8, 8)] = taken.astype(jnp.bfloat16).reshape(8, PAD, 2 * ffw)
        return carry

    lax.fori_loop(0, count // 8, build, 0)
    own_pre = pltpu.make_async_copy(pre.at[me], rpre_ref.at[near, z], own_sem.at[1])
    own_pre.start()

    pre_each(0, lambda copy: copy.start())

    def near_copy(a, source, number, j):
        to = lax.rem(near + j, NEAR)
        src = picks[a].at[source, to]
        if j == 0:
            return pltpu.make_async_copy(src, lands[a].at[near, source], near_l.at[a, number])
        return remote(
            src, lands[a].at[near, source], near_s.at[a, number, j], near_r.at[a, number, j],
            {"blk": at(to, z)},
        )

    def gather(a, source, number):
        rows = own_refs[a][...] if number == 0 else rings[a][source]
        take = rg_ref[source]
        if a == 1:
            take = jnp.where(take.astype(jnp.float32) != 0.0, 1.0, 0.0).astype(jnp.bfloat16)
        taken = jnp.dot(take, rows, preferred_element_type=jnp.float32)
        picks[a][source] = taken.astype(jnp.bfloat16).reshape(NEAR, PAD, taken.shape[1])
        for j in (1, 2, 3, 0):
            near_copy(a, source, number, j).start()

    own_g.wait()
    for a in range(2):
        gather(a, z, 0)
    for k in range(1, RING):
        g_copy(k).wait()
    for k in range(HOPS):
        for a in range(2):
            for way in ways(k):
                hop(a, way, k).wait_recv()
                if way in ways(k + 1) and k + 1 < HOPS:
                    hop(a, way, k + 1).start()
            if a == 1 and k + 1 < HOPS:
                pre_each(k + 1, lambda copy: copy.start())
            if k + 1 < HOPS:
                gather(a, wrap(z - k - 1), 2 * k + 1)
                gather(a, wrap(z + k + 1), 2 * k + 2)
            else:
                gather(a, wrap(z + HOPS), 2 * k + 1)

    own_pre.wait()

    for number in range(HOPS):
        pre_each(number, lambda copy: copy.wait())
    for a in range(2):
        for k in range(HOPS):
            for way in ways(k):
                hop(a, way, k).wait_send()
        for number in range(RING):
            offset = (number + 1) // 2
            source = wrap(z - offset if number % 2 else z + offset)
            for j in range(NEAR):
                near_copy(a, source, number, j).wait()


def fold_kernel(
    ret_ref, g_ref, wg_ref, wu_ref, wd_ref, out_ref, sg_ref, su_ref, sd_ref,
    land, part, ring, own_w, acc, cross, near_s, near_r, near_l, ring_s, ring_r, own_sem, w_s, w_r, x_s, x_r,
):
    near, z = place()
    grp = lax.axis_index("grp")
    side, y = grp // SIDE, lax.rem(grp, SIDE)
    other = 1 - side
    terms, sums = (wg_ref, wu_ref, wd_ref), (sg_ref, su_ref, sd_ref)
    width = sg_ref.shape[1]
    barrier = greet(
        [{"grp": side * SIDE + turn(y + step)} for step in (1, -1)]
        + [{"grp": other * SIDE + y}]
        + [{"blk": at(lax.rem(near + j, NEAR), z)} for j in range(1, NEAR)]
        + [{"blk": at(near, wrap(z + step))} for step in (1, -1)]
    )
    pl.semaphore_wait(barrier, 5 + NEAR - 1)

    def near_copy(number, j):
        offset = (number + 1) // 2
        source = wrap(z - offset if number % 2 else z + offset)
        to = lax.rem(near + j, NEAR)
        src, dst = ret_ref.at[to, source], land.at[source, near]
        if j == 0:
            return pltpu.make_async_copy(src, dst, near_l.at[number])
        return remote(src, dst, near_s.at[number, j], near_r.at[number, j], {"blk": at(to, z)})

    def cols(way, to):
        start = ((other if way == 0 else side) * SIDE + to) * width
        return pl.ds(pl.multiple_of(start, width), width)

    def w_hop(way, k, t):
        step = 1 if way == 0 else -1
        src = terms[t].at[:, cols(way, turn(y - step))] if k == 0 else acc.at[way, k - 1, t]
        return remote(
            src, acc.at[way, k, t], w_s.at[way, k, t], w_r.at[way, k, t],
            {"grp": side * SIDE + turn(y + step)},
        )

    def x_copy(t):
        return remote(acc.at[0, SIDE - 2, t], cross.at[t], x_s.at[t], x_r.at[t], {"grp": other * SIDE + y})

    def own_copy(t):
        return pltpu.make_async_copy(terms[t], own_w.at[t], own_sem.at[t])

    def w_sum(way, k, t):
        step = 1 if way == 0 else -1
        w_hop(way, k, t).wait_recv()
        own = own_w[t, :, cols(way, turn(y - step * (k + 2)))]
        return acc[way, k, t].astype(jnp.float32) + own.astype(jnp.float32)

    def w_turn(k):
        for t in range(3):
            for way in range(2):
                acc[way, k, t] = w_sum(way, k, t).astype(jnp.bfloat16)
                w_hop(way, k + 1, t).start()

    for t in range(3):
        for way in range(2):
            w_hop(way, 0, t).start()
    for number in reversed(range(RING)):
        for j in (1, 2, 3, 0):
            near_copy(number, j).start()
    for t in range(3):
        own_copy(t).start()

    half = out_ref.shape[0] // 2

    def hop(way, k):
        step = 1 if way == 0 else -1
        src, dst = part.at[way, k], ring.at[way, k]
        if k == 0:
            src, dst = src.at[pl.ds(0, half)], dst.at[pl.ds(0, half)]
        return remote(src, dst, ring_s.at[way, k], ring_r.at[way, k], {"blk": at(near, wrap(z + step))})

    def scattered(number):
        offset = (number + 1) // 2
        source = wrap(z - offset if number % 2 else z + offset)
        for j in range(NEAR):
            near_copy(number, j).wait()
        rows = land[source].reshape(NEAR * PAD, out_ref.shape[1])
        return jnp.dot(g_ref[source], rows, preferred_element_type=jnp.float32)

    far = scattered(RING - 1).astype(jnp.bfloat16)
    for way in range(2):
        part[way, 0, 0:half] = far[way * half : (way + 1) * half]
        hop(way, 0).start()
    for t in range(3):
        own_copy(t).wait()
    for k in range(1, HOPS):
        for way in range(2):
            offset = HOPS - k
            own = scattered(2 * offset if way == 0 else 2 * offset - 1)
            hop(way, k - 1).wait_recv()
            if k == 1:
                low = ring[way, 0, 0:half].astype(jnp.float32)
                rows = slice(way * half, (way + 1) * half)
                part[way, k] = own.astype(jnp.bfloat16)
                part[way, k, rows] = (own[rows] + low).astype(jnp.bfloat16)
            else:
                part[way, k] = (own + ring[way, k - 1].astype(jnp.float32)).astype(jnp.bfloat16)
            hop(way, k).start()
        if k == 1:
            w_turn(0)
    w_turn(1)
    own = scattered(0)
    for way in range(2):
        hop(way, HOPS - 1).wait_recv()
        own = own + ring[way, HOPS - 1].astype(jnp.float32)
    out_ref[...] = own.astype(jnp.bfloat16)
    for t in range(3):
        acc[0, SIDE - 2, t] = w_sum(0, SIDE - 2, t).astype(jnp.bfloat16)
        x_copy(t).start()
    for t in range(3):
        mine = w_sum(1, SIDE - 2, t)
        x_copy(t).wait_recv()
        sums[t][...] = (mine + cross[t].astype(jnp.float32)).astype(jnp.bfloat16)
    for way in range(2):
        for k in range(HOPS):
            hop(way, k).wait_send()
        for k in range(SIDE - 1):
            for t in range(3):
                w_hop(way, k, t).wait_send()
    for t in range(3):
        x_copy(t).wait_send()


def spread(d_out, tokens, onehot, route, gate_pre, up_pre):
    rows, width = d_out.shape
    bf16, dma = jnp.bfloat16, pltpu.SemaphoreType.DMA
    vmem, anywhere = pl.BlockSpec(memory_space=pltpu.VMEM), pl.BlockSpec(memory_space=pl.ANY)
    landed = jax.ShapeDtypeStruct((NEAR, RING, PAD, width), bf16)
    choices, ffw = gate_pre.shape[:2]
    return pl.pallas_call(
        spread_kernel,
        out_shape=(
            landed,
            landed,
            jax.ShapeDtypeStruct((NEAR, RING, PAD, 2 * ffw), bf16),
            jax.ShapeDtypeStruct(onehot.shape, bf16),
        ),
        in_specs=[vmem, vmem, vmem, vmem, anywhere, anywhere],
        out_specs=(vmem, vmem, anywhere, vmem),
        scratch_shapes=[
            pltpu.VMEM((2 * ffw, choices * rows), bf16),
            pltpu.VMEM((NEAR * RING, PAD, 2 * ffw), bf16),
            dma((2, choices)),
            pltpu.VMEM((RING, rows, width), bf16),
            pltpu.VMEM((RING, rows, width), bf16),
            pltpu.VMEM((RING, NEAR, PAD, width), bf16),
            pltpu.VMEM((RING, NEAR, PAD, width), bf16),
            dma((2, 2, HOPS)),
            dma((2, 2, HOPS)),
            dma((2, RING, NEAR)),
            dma((2, RING, NEAR)),
            dma((2, RING)),
            dma((RING,)),
            dma((RING,)),
            dma((RING, NEAR)),
            dma((RING, NEAR)),
            dma((2,)),
        ],
        compiler_params=pltpu.CompilerParams(
            collective_id=0, has_side_effects=True, vmem_limit_bytes=48 << 20
        ),
        name="spread",
    )(d_out, tokens, onehot, route, gate_pre, up_pre)


def fold(ret, onehot_t, terms):
    width = ret.shape[-1]
    rows = onehot_t.shape[1]
    bf16, dma = jnp.bfloat16, pltpu.SemaphoreType.DMA
    vmem, anywhere = pl.BlockSpec(memory_space=pltpu.VMEM), pl.BlockSpec(memory_space=pl.ANY)
    ffw = terms[0].shape[0]
    share = (ffw, width // lax.axis_size("grp"))
    return pl.pallas_call(
        fold_kernel,
        out_shape=(jax.ShapeDtypeStruct((rows, width), bf16),) + (jax.ShapeDtypeStruct(share, bf16),) * 3,
        in_specs=[vmem, vmem, anywhere, anywhere, anywhere],
        out_specs=(vmem,) * 4,
        scratch_shapes=[
            pltpu.VMEM((RING, NEAR, PAD, width), bf16),
            pltpu.VMEM((2, HOPS, rows, width), bf16),
            pltpu.VMEM((2, HOPS, rows, width), bf16),
            pltpu.VMEM((3, ffw, width), bf16),
            pltpu.VMEM((2, SIDE - 1, 3) + share, bf16),
            pltpu.VMEM((3,) + share, bf16),
            dma((RING, NEAR)),
            dma((RING, NEAR)),
            dma((RING,)),
            dma((2, HOPS)),
            dma((2, HOPS)),
            dma((3,)),
            dma((2, SIDE - 1, 3)),
            dma((2, SIDE - 1, 3)),
            dma((3,)),
            dma((3,)),
        ],
        compiler_params=pltpu.CompilerParams(
            collective_id=1, has_side_effects=True, vmem_limit_bytes=48 << 20
        ),
        name="fold",
    )(ret, onehot_t, *terms)


def per_device(
    tokens, d_out, expert_ids, gate_values, saved_gate_pre, saved_up_pre, w_gate, w_up, w_down
):
    bf16, f32 = jnp.bfloat16, jnp.float32
    rows, width = tokens.shape
    ffw = saved_gate_pre.shape[2]
    experts = NEAR * RING
    chosen = expert_ids[:, :, None] == jnp.arange(experts, dtype=jnp.int32)[None, None, :]
    hit = jnp.any(chosen, axis=1)
    before = jnp.tril(jnp.ones((rows, rows), bf16), -1)
    rank = jnp.dot(before, hit.astype(bf16), preferred_element_type=f32).astype(jnp.int32)
    slot = jnp.where(hit, rank, PAD).T
    onehot = (slot[:, None, :] == jnp.arange(PAD, dtype=jnp.int32)[None, :, None])
    gate_of = jnp.sum(jnp.where(chosen, gate_values.astype(f32)[:, :, None], 0.0), axis=1).T
    by_z = jnp.where(onehot, gate_of[:, None, :], 0.0).astype(bf16).reshape(2, RING, 2, PAD, rows)
    by_z = jnp.transpose(by_z, (1, 0, 2, 3, 4)).reshape(RING, NEAR * PAD, rows)
    route = (onehot[None] & chosen.transpose(1, 2, 0)[:, :, None, :]).astype(bf16)
    route = route.reshape(-1, experts * PAD, rows)

    recv_d, recv_t, recv_pre, recv_g = spread(
        d_out, tokens, by_z, route, *(jnp.transpose(a, (1, 2, 0)) for a in (saved_gate_pre, saved_up_pre))
    )

    cot = recv_d.reshape(experts * PAD, width)
    inputs = recv_t.reshape(experts * PAD, width)
    recv_pre = recv_pre.reshape(experts * PAD, 2 * ffw)
    gate_pre = recv_pre[:, :ffw].astype(f32)
    up_pre = recv_pre[:, ffw:].astype(f32)
    sig = jax.nn.sigmoid(gate_pre)
    active = gate_pre * sig
    hidden = (active * up_pre).astype(bf16)
    back = jnp.einsum("rd,fd->rf", cot, w_down[0], preferred_element_type=f32)
    grad_gate = (back * up_pre * sig * (1.0 + gate_pre * (1.0 - sig))).astype(bf16)
    grad_up = (back * active).astype(bf16)
    ret = (
        jnp.einsum("rf,df->rd", grad_gate, w_gate[0], preferred_element_type=f32)
        + jnp.einsum("rf,df->rd", grad_up, w_up[0], preferred_element_type=f32)
    ).astype(bf16)
    terms = [
        jnp.einsum("rf,rd->fd", left, right, preferred_element_type=f32).astype(bf16)
        for left, right in ((grad_gate, inputs), (grad_up, inputs), (hidden, cot))
    ]

    d_tokens, sum_gate, sum_up, sum_down = fold(
        ret.reshape(NEAR, RING, PAD, width), jnp.swapaxes(recv_g != 0, 1, 2).astype(bf16), terms
    )
    return (
        d_tokens,
        jnp.swapaxes(sum_gate, 0, 1)[None],
        jnp.swapaxes(sum_up, 0, 1)[None],
        sum_down[None],
    )


def solution(mesh):
    rows = P(("grp", "blk"), None)
    return jax.shard_map(
        per_device,
        mesh=mesh,
        in_specs=(
            rows,
            rows,
            rows,
            rows,
            P(("grp", "blk"), None, None),
            P(("grp", "blk"), None, None),
            P("blk", None, None),
            P("blk", None, None),
            P("blk", None, None),
        ),
        out_specs=(rows, P("blk", "grp", None), P("blk", "grp", None), P("blk", None, "grp")),
        check_vma=False,
    )
```

```python
import jax
import jax.numpy as jnp
from jax import lax
from jax.experimental import pallas as pl
from jax.experimental.pallas import tpu as pltpu
from jax.sharding import PartitionSpec as P

MESH = pl.DeviceIdType.MESH
RING = 8
NEAR = 4
HOPS = RING // 2
PAD = 32
LOW = 64
PRE_STAGES = ((3, 5), (4,), (2, 6), (1, 7, 0))
SIDE = 4


def place():
    me = lax.axis_index("blk")
    return me // (2 * RING) * 2 + lax.rem(me, 2), lax.rem(me // 2, RING)


def at(near, z):
    return near // 2 * (2 * RING) + z * 2 + lax.rem(near, 2)


def wrap(z):
    return lax.rem(z + RING, RING)


def turn(y):
    return lax.rem(y + 2 * SIDE, SIDE)


def greet(peers):
    barrier = pltpu.get_barrier_semaphore()
    for peer in peers:
        pl.semaphore_signal(barrier, inc=1, device_id=peer, device_id_type=MESH)
    return barrier


def remote(src, dst, send, recv, peer):
    return pltpu.make_async_remote_copy(
        src_ref=src, dst_ref=dst, send_sem=send, recv_sem=recv, device_id=peer, device_id_type=MESH
    )


def spread_kernel(
    d_ref, t_ref, g_ref, route_ref, gate_ref, up_ref, rd_ref, rt_ref, rpre_ref, rg_ref,
    table, pre, table_sem, ring_d, ring_t, pick_d, pick_t, ring_s, ring_r, near_s, near_r, near_l, g_s, g_r, pre_s, pre_r, own_sem,
):
    near, z = place()
    me = lax.axis_index("blk")
    count = 2 * 2 * RING
    barrier = pltpu.get_barrier_semaphore()

    def hello(k, carry):
        pl.semaphore_signal(
            barrier, inc=1, device_id={"blk": lax.rem(me + k, count)}, device_id_type=MESH
        )
        return carry

    lax.fori_loop(1, count, hello, 0)
    pl.semaphore_wait(barrier, count - 1)

    own_refs, rings = (d_ref, t_ref), (ring_d, ring_t)
    picks, lands = (pick_d, pick_t), (rd_ref, rt_ref)
    far = pl.ds(0, LOW), pl.ds(LOW, d_ref.shape[0] - LOW)

    def ways(k):
        return [way for way in range(2) if k < HOPS - 1 or far[way].size]

    def hop(a, way, k):
        step = 1 if way == 0 else -1
        source = wrap(z - step * k)
        src = own_refs[a] if k == 0 else rings[a].at[source]
        dst = rings[a].at[source]
        if k == HOPS - 1:
            src = src.at[far[way]]
            dst = dst.at[far[way]]
        return remote(
            src, dst, ring_s.at[a, way, k], ring_r.at[a, way, k], {"blk": at(near, wrap(z + step))}
        )

    def g_copy(k):
        to = wrap(z + k)
        return remote(g_ref.at[to], rg_ref.at[z], g_s.at[k], g_r.at[k], {"blk": at(near, to)})

    def pre_copy(k, j):
        to = at(lax.rem(near + j, NEAR), wrap(z + k))
        return remote(pre.at[to], rpre_ref.at[near, z], pre_s.at[k, j], pre_r.at[k, j], {"blk": to})

    def pre_each(number, act):
        for k in PRE_STAGES[number]:
            def one(j, carry, k=k):
                act(pre_copy(k, j))
                return carry

            lax.fori_loop(0 if k else 1, NEAR, one, 0)

    choices, ffw, rows = gate_ref.shape

    def table_copy(i, k):
        ref = (gate_ref, up_ref)[i]
        dst = table.at[pl.ds(i * ffw, ffw), pl.ds(k * rows, rows)]
        return pltpu.make_async_copy(ref.at[k], dst, table_sem.at[i, k])

    for a in range(2):
        for way in range(2):
            hop(a, way, 0).start()
    for i in range(2):
        for k in range(choices):
            table_copy(i, k).start()
    for k in range(1, RING):
        g_copy(k).start()
    own_g = pltpu.make_async_copy(g_ref.at[z], rg_ref.at[z], own_sem.at[0])
    own_g.start()
    for i in range(2):
        for k in range(choices):
            table_copy(i, k).wait()

    def build(i, carry):
        slots = pl.ds(pl.multiple_of(i * 8 * PAD, 8 * PAD), 8 * PAD)
        take = jnp.concatenate([route_ref[k, slots, :] for k in range(choices)], axis=1)
        taken = lax.dot_general(
            take, table[...], (((1,), (1,)), ((), ())), preferred_element_type=jnp.float32
        )
        pre[pl.ds(i * 8, 8)] = taken.astype(jnp.bfloat16).reshape(8, PAD, 2 * ffw)
        return carry

    lax.fori_loop(0, count // 8, build, 0)
    own_pre = pltpu.make_async_copy(pre.at[me], rpre_ref.at[near, z], own_sem.at[1])
    own_pre.start()

    pre_each(0, lambda copy: copy.start())

    def near_copy(a, source, number, j):
        to = lax.rem(near + j, NEAR)
        src = picks[a].at[source, to]
        if j == 0:
            return pltpu.make_async_copy(src, lands[a].at[near, source], near_l.at[a, number])
        return remote(
            src, lands[a].at[near, source], near_s.at[a, number, j], near_r.at[a, number, j],
            {"blk": at(to, z)},
        )

    def gather(a, source, number):
        rows = own_refs[a][...] if number == 0 else rings[a][source]
        take = rg_ref[source]
        if a == 1:
            take = jnp.where(take.astype(jnp.float32) != 0.0, 1.0, 0.0).astype(jnp.bfloat16)
        taken = jnp.dot(take, rows, preferred_element_type=jnp.float32)
        picks[a][source] = taken.astype(jnp.bfloat16).reshape(NEAR, PAD, taken.shape[1])
        for j in (1, 2, 3, 0):
            near_copy(a, source, number, j).start()

    own_g.wait()
    for a in range(2):
        gather(a, z, 0)
    for k in range(1, RING):
        g_copy(k).wait()
    for k in range(HOPS):
        for a in range(2):
            for way in ways(k):
                hop(a, way, k).wait_recv()
                if way in ways(k + 1) and k + 1 < HOPS:
                    hop(a, way, k + 1).start()
            if a == 1 and k + 1 < HOPS:
                pre_each(k + 1, lambda copy: copy.start())
            if k + 1 < HOPS:
                gather(a, wrap(z - k - 1), 2 * k + 1)
                gather(a, wrap(z + k + 1), 2 * k + 2)
            else:
                gather(a, wrap(z + HOPS), 2 * k + 1)

    own_pre.wait()

    for number in range(HOPS):
        pre_each(number, lambda copy: copy.wait())
    for a in range(2):
        for k in range(HOPS):
            for way in ways(k):
                hop(a, way, k).wait_send()
        for number in range(RING):
            offset = (number + 1) // 2
            source = wrap(z - offset if number % 2 else z + offset)
            for j in range(NEAR):
                near_copy(a, source, number, j).wait()


def fold_kernel(
    ret_ref, g_ref, wg_ref, wu_ref, wd_ref, out_ref, sg_ref, su_ref, sd_ref,
    land, part, ring, own_w, acc, cross, near_s, near_r, near_l, ring_s, ring_r, own_sem, w_s, w_r, x_s, x_r,
):
    near, z = place()
    grp = lax.axis_index("grp")
    side, y = grp // SIDE, lax.rem(grp, SIDE)
    other = 1 - side
    terms, sums = (wg_ref, wu_ref, wd_ref), (sg_ref, su_ref, sd_ref)
    width = sg_ref.shape[1]
    barrier = greet(
        [{"grp": side * SIDE + turn(y + step)} for step in (1, -1)]
        + [{"grp": other * SIDE + y}]
        + [{"blk": at(lax.rem(near + j, NEAR), z)} for j in range(1, NEAR)]
        + [{"blk": at(near, wrap(z + step))} for step in (1, -1)]
    )
    pl.semaphore_wait(barrier, 5 + NEAR - 1)

    def near_copy(number, j):
        offset = (number + 1) // 2
        source = wrap(z - offset if number % 2 else z + offset)
        to = lax.rem(near + j, NEAR)
        src, dst = ret_ref.at[to, source], land.at[source, near]
        if j == 0:
            return pltpu.make_async_copy(src, dst, near_l.at[number])
        return remote(src, dst, near_s.at[number, j], near_r.at[number, j], {"blk": at(to, z)})

    def cols(way, to):
        start = ((other if way == 0 else side) * SIDE + to) * width
        return pl.ds(pl.multiple_of(start, width), width)

    def w_hop(way, k, t):
        step = 1 if way == 0 else -1
        src = terms[t].at[:, cols(way, turn(y - step))] if k == 0 else acc.at[way, k - 1, t]
        return remote(
            src, acc.at[way, k, t], w_s.at[way, k, t], w_r.at[way, k, t],
            {"grp": side * SIDE + turn(y + step)},
        )

    def x_copy(t):
        return remote(acc.at[0, SIDE - 2, t], cross.at[t], x_s.at[t], x_r.at[t], {"grp": other * SIDE + y})

    def own_copy(t):
        return pltpu.make_async_copy(terms[t], own_w.at[t], own_sem.at[t])

    def w_sum(way, k, t):
        step = 1 if way == 0 else -1
        w_hop(way, k, t).wait_recv()
        own = own_w[t, :, cols(way, turn(y - step * (k + 2)))]
        return acc[way, k, t].astype(jnp.float32) + own.astype(jnp.float32)

    def w_turn(k):
        for t in range(3):
            for way in range(2):
                acc[way, k, t] = w_sum(way, k, t).astype(jnp.bfloat16)
                w_hop(way, k + 1, t).start()

    for t in range(3):
        for way in range(2):
            w_hop(way, 0, t).start()
    for number in reversed(range(RING)):
        for j in (1, 2, 3, 0):
            near_copy(number, j).start()
    for t in range(3):
        own_copy(t).start()

    half = out_ref.shape[0] // 2

    def hop(way, k):
        step = 1 if way == 0 else -1
        src, dst = part.at[way, k], ring.at[way, k]
        if k == 0:
            src, dst = src.at[pl.ds(0, half)], dst.at[pl.ds(0, half)]
        return remote(src, dst, ring_s.at[way, k], ring_r.at[way, k], {"blk": at(near, wrap(z + step))})

    def scattered(number):
        offset = (number + 1) // 2
        source = wrap(z - offset if number % 2 else z + offset)
        for j in range(NEAR):
            near_copy(number, j).wait()
        rows = land[source].reshape(NEAR * PAD, out_ref.shape[1])
        return jnp.dot(g_ref[source], rows, preferred_element_type=jnp.float32)

    far = scattered(RING - 1).astype(jnp.bfloat16)
    for way in range(2):
        part[way, 0, 0:half] = far[way * half : (way + 1) * half]
        hop(way, 0).start()
    for t in range(3):
        own_copy(t).wait()
    for k in range(1, HOPS):
        for way in range(2):
            offset = HOPS - k
            own = scattered(2 * offset if way == 0 else 2 * offset - 1)
            hop(way, k - 1).wait_recv()
            if k == 1:
                low = ring[way, 0, 0:half].astype(jnp.float32)
                rows = slice(way * half, (way + 1) * half)
                part[way, k] = own.astype(jnp.bfloat16)
                part[way, k, rows] = (own[rows] + low).astype(jnp.bfloat16)
            else:
                part[way, k] = (own + ring[way, k - 1].astype(jnp.float32)).astype(jnp.bfloat16)
            hop(way, k).start()
        if k == 1:
            w_turn(0)
    w_turn(1)
    own = scattered(0)
    for way in range(2):
        hop(way, HOPS - 1).wait_recv()
        own = own + ring[way, HOPS - 1].astype(jnp.float32)
    out_ref[...] = own.astype(jnp.bfloat16)
    for t in range(3):
        acc[0, SIDE - 2, t] = w_sum(0, SIDE - 2, t).astype(jnp.bfloat16)
        x_copy(t).start()
    for t in range(3):
        mine = w_sum(1, SIDE - 2, t)
        x_copy(t).wait_recv()
        sums[t][...] = (mine + cross[t].astype(jnp.float32)).astype(jnp.bfloat16)
    for way in range(2):
        for k in range(HOPS):
            hop(way, k).wait_send()
        for k in range(SIDE - 1):
            for t in range(3):
                w_hop(way, k, t).wait_send()
    for t in range(3):
        x_copy(t).wait_send()


def spread(d_out, tokens, onehot, route, gate_pre, up_pre):
    rows, width = d_out.shape
    bf16, dma = jnp.bfloat16, pltpu.SemaphoreType.DMA
    vmem, anywhere = pl.BlockSpec(memory_space=pltpu.VMEM), pl.BlockSpec(memory_space=pl.ANY)
    landed = jax.ShapeDtypeStruct((NEAR, RING, PAD, width), bf16)
    choices, ffw = gate_pre.shape[:2]
    return pl.pallas_call(
        spread_kernel,
        out_shape=(
            landed,
            landed,
            jax.ShapeDtypeStruct((NEAR, RING, PAD, 2 * ffw), bf16),
            jax.ShapeDtypeStruct(onehot.shape, bf16),
        ),
        in_specs=[vmem, vmem, vmem, vmem, anywhere, anywhere],
        out_specs=(vmem, vmem, anywhere, vmem),
        scratch_shapes=[
            pltpu.VMEM((2 * ffw, choices * rows), bf16),
            pltpu.VMEM((NEAR * RING, PAD, 2 * ffw), bf16),
            dma((2, choices)),
            pltpu.VMEM((RING, rows, width), bf16),
            pltpu.VMEM((RING, rows, width), bf16),
            pltpu.VMEM((RING, NEAR, PAD, width), bf16),
            pltpu.VMEM((RING, NEAR, PAD, width), bf16),
            dma((2, 2, HOPS)),
            dma((2, 2, HOPS)),
            dma((2, RING, NEAR)),
            dma((2, RING, NEAR)),
            dma((2, RING)),
            dma((RING,)),
            dma((RING,)),
            dma((RING, NEAR)),
            dma((RING, NEAR)),
            dma((2,)),
        ],
        compiler_params=pltpu.CompilerParams(
            collective_id=0, has_side_effects=True, vmem_limit_bytes=48 << 20
        ),
        name="spread",
    )(d_out, tokens, onehot, route, gate_pre, up_pre)


def fold(ret, onehot_t, terms):
    width = ret.shape[-1]
    rows = onehot_t.shape[1]
    bf16, dma = jnp.bfloat16, pltpu.SemaphoreType.DMA
    vmem, anywhere = pl.BlockSpec(memory_space=pltpu.VMEM), pl.BlockSpec(memory_space=pl.ANY)
    ffw = terms[0].shape[0]
    share = (ffw, width // lax.axis_size("grp"))
    return pl.pallas_call(
        fold_kernel,
        out_shape=(jax.ShapeDtypeStruct((rows, width), bf16),) + (jax.ShapeDtypeStruct(share, bf16),) * 3,
        in_specs=[vmem, vmem, anywhere, anywhere, anywhere],
        out_specs=(vmem,) * 4,
        scratch_shapes=[
            pltpu.VMEM((RING, NEAR, PAD, width), bf16),
            pltpu.VMEM((2, HOPS, rows, width), bf16),
            pltpu.VMEM((2, HOPS, rows, width), bf16),
            pltpu.VMEM((3, ffw, width), bf16),
            pltpu.VMEM((2, SIDE - 1, 3) + share, bf16),
            pltpu.VMEM((3,) + share, bf16),
            dma((RING, NEAR)),
            dma((RING, NEAR)),
            dma((RING,)),
            dma((2, HOPS)),
            dma((2, HOPS)),
            dma((3,)),
            dma((2, SIDE - 1, 3)),
            dma((2, SIDE - 1, 3)),
            dma((3,)),
            dma((3,)),
        ],
        compiler_params=pltpu.CompilerParams(
            collective_id=1, has_side_effects=True, vmem_limit_bytes=48 << 20
        ),
        name="fold",
    )(ret, onehot_t, *terms)


def per_device(
    tokens, d_out, expert_ids, gate_values, saved_gate_pre, saved_up_pre, w_gate, w_up, w_down
):
    bf16, f32 = jnp.bfloat16, jnp.float32
    rows, width = tokens.shape
    ffw = saved_gate_pre.shape[2]
    experts = NEAR * RING
    chosen = expert_ids[:, :, None] == jnp.arange(experts, dtype=jnp.int32)[None, None, :]
    hit = jnp.any(chosen, axis=1)
    before = jnp.tril(jnp.ones((rows, rows), bf16), -1)
    rank = jnp.dot(before, hit.astype(bf16), preferred_element_type=f32).astype(jnp.int32)
    slot = jnp.where(hit, rank, PAD).T
    onehot = (slot[:, None, :] == jnp.arange(PAD, dtype=jnp.int32)[None, :, None])
    gate_of = jnp.sum(jnp.where(chosen, gate_values.astype(f32)[:, :, None], 0.0), axis=1).T
    by_z = jnp.where(onehot, gate_of[:, None, :], 0.0).astype(bf16).reshape(2, RING, 2, PAD, rows)
    by_z = jnp.transpose(by_z, (1, 0, 2, 3, 4)).reshape(RING, NEAR * PAD, rows)
    route = (onehot[None] & chosen.transpose(1, 2, 0)[:, :, None, :]).astype(bf16)
    route = route.reshape(-1, experts * PAD, rows)

    recv_d, recv_t, recv_pre, recv_g = spread(
        d_out, tokens, by_z, route, *(jnp.transpose(a, (1, 2, 0)) for a in (saved_gate_pre, saved_up_pre))
    )

    cot = recv_d.reshape(experts * PAD, width)
    inputs = recv_t.reshape(experts * PAD, width)
    recv_pre = recv_pre.reshape(experts * PAD, 2 * ffw).T
    gate_pre = recv_pre[:ffw].astype(f32)
    up_pre = recv_pre[ffw:].astype(f32)
    sig = jax.nn.sigmoid(gate_pre)
    active = gate_pre * sig
    hidden = (active * up_pre).astype(bf16)
    back = jnp.einsum("fd,rd->fr", w_down[0], cot, preferred_element_type=f32)
    grad_gate = (back * up_pre * sig * (1.0 + gate_pre * (1.0 - sig))).astype(bf16)
    grad_up = (back * active).astype(bf16)
    ret = (
        jnp.einsum("fr,df->rd", grad_gate, w_gate[0], preferred_element_type=f32)
        + jnp.einsum("fr,df->rd", grad_up, w_up[0], preferred_element_type=f32)
    ).astype(bf16)
    terms = [
        jnp.einsum("fr,rd->fd", left, right, preferred_element_type=f32).astype(bf16)
        for left, right in ((grad_gate, inputs), (grad_up, inputs), (hidden, cot))
    ]

    d_tokens, sum_gate, sum_up, sum_down = fold(
        ret.reshape(NEAR, RING, PAD, width), jnp.swapaxes(recv_g != 0, 1, 2).astype(bf16), terms
    )
    return (
        d_tokens,
        jnp.swapaxes(sum_gate, 0, 1)[None],
        jnp.swapaxes(sum_up, 0, 1)[None],
        sum_down[None],
    )


def solution(mesh):
    rows = P(("grp", "blk"), None)
    return jax.shard_map(
        per_device,
        mesh=mesh,
        in_specs=(
            rows,
            rows,
            rows,
            rows,
            P(("grp", "blk"), None, None),
            P(("grp", "blk"), None, None),
            P("blk", None, None),
            P("blk", None, None),
            P("blk", None, None),
        ),
        out_specs=(rows, P("blk", "grp", None), P("blk", "grp", None), P("blk", None, "grp")),
        check_vma=False,
    )
```
